32 devices in a mesh: atm: 8 (over y, x, core), ocn: 4 (over z).
Axes of the slice: x: 2, y: 2, z: 4, core: 2. Of those that a mesh axis runs over, the one named last changes fastest.
Arguments:
- prior_states: bfloat16 [256, 8, 256], P(('atm', 'ocn')), may hold values from -6 to 6
- patch_mesh_location: int32 [256], P(('atm', 'ocn')), may hold values from 0 to 65535
- fetched_blocks: int32 [256, 5], P(('atm', 'ocn')), may hold values from 0 to 31, all different within a row; in each aligned block of 8 rows (0 to 7, 8 to 15, ...) at most 2 rows name the same one
- measured_deviations: bfloat16 [16384, 256], P(('atm', 'ocn')), may hold values from -6 to 6
- departure_vectors: float32 [16384, 256], P(('atm', 'ocn')), may hold values from -16 to 16
- measurement_error_spread: float32 [16384], P(('atm', 'ocn')), may hold values from 4 to 8
- measurement_mesh_location: int32 [16384], P(('atm', 'ocn')), may hold values from 0 to 65535
Outputs:
- analysis: float32 [256, 8, 256], P(('atm', 'ocn'))
The draws below stay inside these ranges and needn't reach their ends.
Inputs may be any that keep to these rules, and one draw needn't show every extreme that they name: `fetched_blocks`: each tile names 5 different blocks; among the tiles of one device no block is named by more than 2 tiles, and some block is named by exactly 2 of them.
All inputs are finite; a program needn't handle non-finite values.
Results may differ from the reference program's by a relative error of at most 0.00055.
The reference program's roundings to bfloat16 on the way count: a program that leaves them out, or rounds other values in their place, can miss the bound.
Values may be sent and summed in bfloat16 or wider, within the bound.
No kernel may reach another device: no remote copies, remote signals or barrier semaphores. Data moves between devices by JAX's collectives and lax.ppermute only.
A program may use at most 64 MiB of HBM per device.

```python
import math
import jax
import jax.numpy as jnp
import numpy as np
from jax import lax

TRAJECTORY_TOTAL = 256
OBS_BLOCK = 512
READS = 5
CAP = 2
SWEEPS = 2
GRID = 65536
STATE_LINES_EACH = 8
LENGTH = 16384
NBLOCKS = 32
NOBS = 16384
TILES_DEV = 8
PATCH_TOTAL = 256


def draw_measured_deviations(key, part):
    element_numbers = jnp.clip(jax.random.normal(key, (NOBS, TRAJECTORY_TOTAL), jnp.float32), -6.0, 6.0)
    return element_numbers.astype(jnp.bfloat16)


def with_ends(values, own_key, smallest, top_value):
    shape = values.shape
    spot = [jax.random.randint(jax.random.fold_in(own_key, axis), (), 0, shape[axis]) for axis in range(len(shape))]
    values = values.at[tuple(spot)].set(smallest)
    longest = shape.index(max(shape))
    spot[longest] = (spot[longest] + 1) % shape[longest]
    return values.at[tuple(spot)].set(top_value)


def steps_of(own_key, dims, pieces, low, largest):
    def one(dim, shards_of):
        draws = jax.random.uniform(jax.random.fold_in(jax.random.fold_in(own_key, 6), dim), (shards_of,), jnp.float32, low / len(pieces), largest / len(pieces))
        return jnp.repeat(jnp.exp(draws), dims[dim] // shards_of).reshape((-1,) + (1,) * (len(dims) - dim - 1))

    gain = one(*pieces[0])
    for cut in pieces[1:]:
        gain = gain * one(*cut)
    return gain


def assign_block(rng, own, number, rows, amount, top, limit, lean):
    order = jax.random.permutation(rng, amount)
    heavy_load, ordinary = shares(amount, rows * top, limit, lean, True), shares(amount, rows * top, limit, lean, False)
    places = jnp.arange(amount)

    def named(tallies, turn):
        used = int((tallies > 0).sum())
        fixed = max(1, used // 4)
        passed = fixed + (places - fixed + turn * (used - fixed)) % max(1, amount - fixed)
        return jnp.zeros((amount,), jnp.int32).at[order[jnp.where(places < fixed, places, passed)]].set(jnp.asarray(tallies, jnp.int32))

    tallies = jnp.where(number % 4 == 0, named(heavy_load, number // 4), named(ordinary, number - number // 4 - 1))
    mixed = jax.random.permutation(jax.random.fold_in(own, 3), amount)
    source_of, receiver = mixed[0:amount // 2 * 2:2], mixed[1:amount // 2 * 2:2]
    room = jnp.minimum(tallies[source_of] - 1, limit - tallies[receiver]) // 2
    room = jnp.where((source_of == order[0]) | (receiver == order[0]) | (tallies[receiver] == 0), 0, jnp.maximum(room, 0))
    passed = jax.random.randint(jax.random.fold_in(own, 4), (amount // 2,), 0, 1 << 20) % (room + 1)
    tallies = tallies.at[source_of].add(-passed).at[receiver].add(passed)
    items = jnp.searchsorted(jnp.cumsum(tallies), jnp.arange(rows * top), side="right").astype(jnp.int32)
    grid = items.reshape(top, rows).T
    grid = grid[jax.random.permutation(jax.random.fold_in(own, 1), rows)]
    turn = jax.random.randint(jax.random.fold_in(own, 2), (rows, 1), 0, top)
    return jnp.take_along_axis(grid, (jnp.arange(top)[None, :] + turn) % top, axis=1)


def shares(number_of, total, reach, skew, full):
    weights = [(1 << 20) // math.isqrt(rank ** skew) + 1 for rank in range(1, number_of + 1)]
    largest = reach if full else min(reach, max(-(-total // number_of), total * weights[0] // sum(weights)))
    least = 1 if total - largest >= number_of - 1 else 0
    counts, spare = [largest] + [least] * (number_of - 1), total - largest - least * (number_of - 1)
    while spare > 0:
        movable = [i for i in range(1, number_of) if counts[i] < largest] or [i for i in range(1, number_of) if counts[i] < reach]
        whole, budget = sum([weights[i] for i in movable]), spare
        for i in movable:
            more = min(reach - counts[i], max(1, budget * weights[i] // whole), spare)
            counts[i] = counts[i] + more
            spare = spare - more
    return np.array(counts)


def scatter_about(key, dims, scale, limit, split=(), held_as=jnp.bfloat16):
    factor_of = steps_of(key, dims, split, -0.22, 0.18) if split else 1.0
    result = jax.random.normal(key, dims, jnp.float32) * scale * factor_of
    return jnp.minimum(jnp.maximum(result, -limit), limit).astype(held_as)


def setup_inputs(seed: int = 0) -> dict:
    splits = jax.random.split(jax.random.key(seed), 8)
    prior_states = scatter_about(splits[0], (PATCH_TOTAL, STATE_LINES_EACH, TRAJECTORY_TOTAL), 1.0, 6.0, ((0, 32),))
    patch_mesh_location = with_ends(jax.random.randint(splits[1], (PATCH_TOTAL,), 0, GRID), jax.random.fold_in(splits[1], 1), 0, GRID - 1).astype(jnp.int32)
    fetched_blocks_keys = jax.random.split(jax.random.fold_in(splits[2], 1), PATCH_TOTAL // TILES_DEV)
    fetched_blocks_turns = jax.random.permutation(jax.random.fold_in(splits[2], 3), PATCH_TOTAL // TILES_DEV)
    fetched_blocks = jax.vmap(lambda own, number: assign_block(jax.random.fold_in(splits[2], 2), own, number, TILES_DEV, NBLOCKS, READS, CAP, 2))(fetched_blocks_keys, fetched_blocks_turns).reshape((PATCH_TOTAL, READS))
    measured_deviations = draw_measured_deviations(jax.random.fold_in(splits[7], 71), 0)
    departure_vectors = scatter_about(splits[4], (NOBS, TRAJECTORY_TOTAL), 3.0, 16.0, ((0, 32),), jnp.float32)
    measurement_error_spread = jnp.clip(jnp.exp(math.log(8.0) - 0.6931472 * jax.random.uniform(splits[5], (NOBS,), jnp.float32) ** steps_of(splits[5], (NOBS,), ((0, 32),), -0.2, 0.2)), 4.0, 8.0)
    measurement_mesh_location = with_ends(jax.random.randint(splits[6], (NOBS,), 0, GRID), jax.random.fold_in(splits[6], 1), 0, GRID - 1).astype(jnp.int32)
    return dict(prior_states=prior_states, patch_mesh_location=patch_mesh_location, fetched_blocks=fetched_blocks, measured_deviations=measured_deviations, departure_vectors=departure_vectors, measurement_error_spread=measurement_error_spread, measurement_mesh_location=measurement_mesh_location)


def taper(first, second):
    spread = (first - second).astype(jnp.float32) / LENGTH
    return 1.0 / (1.0 + spread * spread)


def reference(prior_states, patch_mesh_location, fetched_blocks, measured_deviations, departure_vectors, measurement_error_spread, measurement_mesh_location):
    sampled_trajectories = prior_states.shape[2]
    inverse = 1.0 / (sampled_trajectories - 1)
    blocks_y = measured_deviations.reshape(NBLOCKS, OBS_BLOCK, sampled_trajectories)
    blocks_q = measurement_mesh_location.reshape(NBLOCKS, OBS_BLOCK).astype(jnp.int32)
    zero_y = jnp.zeros((1, OBS_BLOCK, sampled_trajectories), measured_deviations.dtype)
    zero_q = jnp.zeros((1, OBS_BLOCK), jnp.int32)
    padded_y = jnp.concatenate([zero_y, blocks_y, zero_y], axis=0)
    padded_q = jnp.concatenate([zero_q, blocks_q, zero_q], axis=0)

    def tapered_cross(index):
        own_rows = lax.dynamic_index_in_dim(blocks_y, index, 0, keepdims=False)
        own_q = lax.dynamic_index_in_dim(blocks_q, index, 0, keepdims=False)
        near_rows = lax.dynamic_slice_in_dim(padded_y, index, 3, 0).reshape(3 * OBS_BLOCK, sampled_trajectories)
        near_q = lax.dynamic_slice_in_dim(padded_q, index, 3, 0).reshape(3 * OBS_BLOCK)
        product = jnp.dot(own_rows, near_rows.T, preferred_element_type=jnp.float32)
        return product * inverse * taper(own_q[:, None], near_q[None, :])

    floats_y = blocks_y.astype(jnp.float32)
    diagonal = jnp.sum(floats_y * floats_y, axis=2) * inverse
    target = departure_vectors.reshape(NBLOCKS, OBS_BLOCK, sampled_trajectories)
    errors = measurement_error_spread.reshape(NBLOCKS, OBS_BLOCK, 1)
    divisor = diagonal[:, :, None] + errors
    weights = target / divisor
    block_ids = jnp.arange(NBLOCKS, dtype=jnp.int32)
    for repeat in range(SWEEPS):
        zero_w = jnp.zeros((1, OBS_BLOCK, sampled_trajectories), weights.dtype)
        padded_w = jnp.concatenate([zero_w, weights, zero_w], axis=0)

        def apply_block(index):
            near_w = lax.dynamic_slice_in_dim(padded_w, index, 3, 0).reshape(3 * OBS_BLOCK, sampled_trajectories)
            return jnp.dot(tapered_cross(index), near_w, precision=lax.Precision.HIGHEST, preferred_element_type=jnp.float32)

        applied = lax.map(apply_block, block_ids) + errors * weights
        weights = weights + (target - applied) / divisor

    weight_rows = lax.optimization_barrier(weights.astype(jnp.bfloat16))
    element_numbers = prior_states.astype(jnp.float32)
    anomalies = lax.optimization_barrier((element_numbers - jnp.mean(element_numbers, axis=2, keepdims=True)).astype(jnp.bfloat16))
    groups = PATCH_TOTAL // 16

    def tile_group(inputs):
        tile_part, place_part, read_part = inputs
        read_y = jnp.take(blocks_y, read_part, axis=0).astype(jnp.float32)
        read_q = jnp.take(blocks_q, read_part, axis=0)
        read_w = jnp.take(weight_rows, read_part, axis=0).astype(jnp.float32)
        product = jnp.einsum("grm,gkjm->gkrj", tile_part.astype(jnp.float32), read_y)
        tapered = product * inverse * taper(place_part[:, None, None, None], read_q[:, :, None, :])
        tapered = lax.optimization_barrier(tapered.astype(jnp.bfloat16)).astype(jnp.float32)
        return jnp.einsum("gkrj,gkjm->grm", tapered, read_w)

    increment = lax.map(tile_group, (anomalies.reshape(groups, 16, STATE_LINES_EACH, sampled_trajectories), patch_mesh_location.astype(jnp.int32).reshape(groups, 16), fetched_blocks.astype(jnp.int32).reshape(groups, 16, READS)))
    return element_numbers + increment.reshape(element_numbers.shape)
```

```python
import functools

import jax
import jax.numpy as jnp
import numpy as np
from jax import lax
from jax.experimental import pallas as pl
from jax.experimental.pallas import tpu as pltpu
from jax.sharding import PartitionSpec as P

OBS_BLOCK = 512
READS = 5
CAP = 2
SWEEPS = 2
LENGTH = 16384
LANES = 128
PARTS = OBS_BLOCK // LANES
AXES = ("atm", "ocn")
RELOCATE = True


def homes(atm, ocn):
    places = []
    for column in range(atm // 2):
        chips = range(ocn) if column % 2 == 0 else range(ocn - 1, -1, -1)
        for chip in chips:
            for core in range(2):
                places.append((2 * column + core) * ocn + chip)
    return places


def as_row(ref, start):
    return jnp.concatenate([ref[start + i : start + i + 1, :] for i in range(PARTS)], axis=1)


def as_column(ref, start, part):
    shape = (LANES, LANES)
    diagonal = lax.broadcasted_iota(jnp.int32, shape, 0) == lax.broadcasted_iota(jnp.int32, shape, 1)
    row = jnp.broadcast_to(ref[start + part : start + part + 1, :], shape)
    return jnp.sum(jnp.where(diagonal, row, 0.0), axis=1, keepdims=True)


def split(values):
    high = values.astype(jnp.bfloat16)
    return high, (values - high.astype(jnp.float32)).astype(jnp.bfloat16)


def start_kernel(inverse, y_ref, meta_ref, target_ref, weights_ref):
    for part in range(PARTS):
        rows = pl.ds(part * LANES, LANES)
        y = y_ref[rows, :].astype(jnp.float32)
        divisor = jnp.sum(y * y, axis=1, keepdims=True) * inverse + as_column(meta_ref, PARTS, part)
        weights_ref[rows, :] = target_ref[rows, :] / divisor


def couple_kernel(inverse, ends_ref, y_ref, before_ref, after_ref, meta_ref, meta_before_ref, meta_after_ref, high_ref, low_ref):
    neighbours = ((before_ref, meta_before_ref, ends_ref[0]), (y_ref, meta_ref, 1), (after_ref, meta_after_ref, ends_ref[1]))
    for part in range(PARTS):
        rows = pl.ds(part * LANES, LANES)
        y = y_ref[rows, :]
        wide = y.astype(jnp.float32)
        divisor = jnp.sum(wide * wide, axis=1, keepdims=True) * inverse + as_column(meta_ref, PARTS, part)
        place = as_column(meta_ref, 0, part)
        for number, (other_ref, other_meta_ref, present) in enumerate(neighbours):
            product = lax.dot_general(
                y, other_ref[...], (((1,), (1,)), ((), ())), preferred_element_type=jnp.float32
            )
            spread = (place - as_row(other_meta_ref, 0)) * (1.0 / LENGTH)
            coupling = product * (-inverse / (divisor * (1.0 + spread * spread)))
            if number == 1:
                shape = (LANES, OBS_BLOCK)
                own = lax.broadcasted_iota(jnp.int32, shape, 0) + part * LANES
                coupling = jnp.where(own == lax.broadcasted_iota(jnp.int32, shape, 1), 0.0, coupling)
            else:
                coupling = jnp.where(present > 0, coupling, 0.0)
            high, low = split(coupling)
            columns = pl.ds(number * OBS_BLOCK, OBS_BLOCK)
            high_ref[rows, columns] = high
            low_ref[rows, columns] = low


def coupled(high_ref, low_ref, before_ref, own_ref, after_ref):
    total = None
    for number, ref in enumerate((before_ref, own_ref, after_ref)):
        high, low = split(ref[...])
        columns = pl.ds(number * OBS_BLOCK, OBS_BLOCK)
        for left, right in ((high_ref, high), (low_ref, high), (high_ref, low)):
            term = jnp.dot(left[:, columns], right, preferred_element_type=jnp.float32)
            total = term if total is None else total + term
    return total


def sweep_kernel(high_ref, low_ref, start_ref, before_ref, own_ref, after_ref, weights_ref):
    weights_ref[...] = start_ref[...] + coupled(high_ref, low_ref, before_ref, own_ref, after_ref)


def answer_kernel(high_ref, low_ref, start_ref, before_ref, own_ref, after_ref, gain_ref, answer_ref):
    weights = start_ref[...] + coupled(high_ref, low_ref, before_ref, own_ref, after_ref)
    answer_ref[...] = jnp.dot(
        gain_ref[...], weights.astype(jnp.bfloat16), preferred_element_type=jnp.float32
    )


def gain_kernel(inverse, lines, place_ref, rows_ref, y_ref, meta_ref, gain_ref, product_ref):
    product_ref[...] = lax.dot_general(
        rows_ref[...], y_ref[...], (((1,), (1,)), ((), ())), preferred_element_type=jnp.float32
    )
    height = CAP * lines
    here = jnp.broadcast_to(as_row(meta_ref, 0), (height, OBS_BLOCK))
    slot = lax.broadcasted_iota(jnp.int32, (height, OBS_BLOCK), 0) // lines

    def group(number, carry):
        rows = pl.ds(pl.multiple_of(number * height, height), height)
        place = jnp.full((height, OBS_BLOCK), place_ref[number * CAP], jnp.int32)
        for extra in range(1, CAP):
            place = jnp.where(slot == extra, place_ref[number * CAP + extra], place)
        spread = (place.astype(jnp.float32) - here) * (1.0 / LENGTH)
        gain = product_ref[rows, :] * inverse / (1.0 + spread * spread)
        gain_ref[rows, :] = gain.astype(jnp.bfloat16)
        return carry

    lax.fori_loop(0, gain_ref.shape[0] // height, group, 0, unroll=2)


def request_kernel(home_ref, reads_ref, place_ref, prior_ref, send_ref, send_place_ref, slot_ref, count_ref):
    tiles, lines, members = prior_ref.shape
    slots = send_ref.shape[0]
    send_ref[...] = jnp.zeros_like(send_ref)

    def clear(number, carry):
        for extra in range(CAP):
            send_place_ref[number * CAP + extra] = 0
        count_ref[number] = 0
        return carry

    lax.fori_loop(0, slots // CAP, clear, 0)

    def tile(number, carry):
        states = prior_ref[number].astype(jnp.float32)
        mean = jnp.sum(states, axis=1, keepdims=True) * (1.0 / members)
        anomalies = (states - mean).astype(send_ref.dtype)
        for read in range(READS):
            block = home_ref[reads_ref[number * READS + read]]
            used = count_ref[block]
            count_ref[block] = used + 1
            slot = block * CAP + jnp.minimum(used, CAP - 1)
            send_ref[slot] = anomalies
            send_place_ref[slot] = place_ref[number]
            slot_ref[number * READS + read] = slot
        return carry

    lax.fori_loop(0, tiles, tile, 0)


def collect_kernel(slot_ref, prior_ref, returned_ref, out_ref):
    def tile(number, carry):
        total = returned_ref[slot_ref[number * READS]]
        for read in range(1, READS):
            total = total + returned_ref[slot_ref[number * READS + read]]
        out_ref[number] = prior_ref[number].astype(jnp.float32) + total
        return carry

    lax.fori_loop(0, prior_ref.shape[0], tile, 0)


VMEM = pl.BlockSpec(memory_space=pltpu.VMEM)
SMEM = pl.BlockSpec(memory_space=pltpu.SMEM)


def call(kernel, ins, outs, name, scratch=()):
    shapes = [jax.ShapeDtypeStruct(shape, dtype) for shape, dtype, _ in outs]
    specs = [space for _, _, space in outs]
    single = len(outs) == 1
    return pl.pallas_call(
        kernel,
        in_specs=list(ins),
        out_shape=shapes[0] if single else shapes,
        out_specs=specs[0] if single else specs,
        scratch_shapes=list(scratch),
        name=name,
    )


def shards(
    home,
    prior_states,
    patch_mesh_location,
    fetched_blocks,
    measured_deviations,
    departure_vectors,
    measurement_error_spread,
    measurement_mesh_location,
):
    f32, bf16, i32 = jnp.float32, jnp.bfloat16, jnp.int32
    tiles, lines, members = prior_states.shape
    inverse = 1.0 / (members - 1)
    devices = len(home)
    slots = devices * CAP
    rows = slots * lines
    up = [(home[k], home[(k + 1) % devices]) for k in range(devices)]
    down = [(b, a) for a, b in up]
    move = [(k, home[k]) for k in range(devices)]
    block_of = np.argsort(np.array(home))
    relocated = home != list(range(devices))

    def send(values, pairs):
        return lax.ppermute(values, AXES, pairs)

    def relocate(values):
        return send(values, move) if relocated else values

    square = (OBS_BLOCK, members)
    meta = jnp.concatenate(
        [measurement_mesh_location.astype(f32), measurement_error_spread]
    ).reshape(2 * PARTS, LANES)
    y = relocate(measured_deviations)
    start = call(
        functools.partial(start_kernel, inverse), [VMEM] * 3, [(square, f32, VMEM)], "start"
    )(measured_deviations, meta, departure_vectors)
    meta = relocate(meta)
    start = relocate(start)

    y_before, y_after = send(y, up), send(y, down)
    meta_before, meta_after = send(meta, up), send(meta, down)
    w_before, w_after = send(start, up), send(start, down)

    send_rows, send_places, slot = call(
        request_kernel,
        [SMEM, SMEM, SMEM, VMEM],
        [((slots, lines, members), bf16, VMEM), ((slots,), i32, SMEM), ((tiles * READS,), i32, SMEM)],
        "request",
        [pltpu.SMEM((devices,), i32)],
    )(jnp.asarray(home, i32), fetched_blocks.reshape(-1), patch_mesh_location, prior_states)
    places = lax.all_to_all(send_places.reshape(devices, 1, CAP), AXES, 0, 0, tiled=True)
    arrived = lax.all_to_all(
        send_rows.reshape(devices, CAP, lines, members), AXES, 0, 0, tiled=True
    )

    me = lax.axis_index(AXES)
    here = jnp.asarray(block_of, i32)[me]
    ends = jnp.stack([here, devices - 1 - here])
    wide = (OBS_BLOCK, 3 * OBS_BLOCK)
    high, low = call(
        functools.partial(couple_kernel, inverse),
        [SMEM] + [VMEM] * 6,
        [(wide, bf16, VMEM), (wide, bf16, VMEM)],
        "couple",
    )(ends, y, y_before, y_after, meta, meta_before, meta_after)
    gain = call(
        functools.partial(gain_kernel, inverse, lines),
        [SMEM] + [VMEM] * 3,
        [((rows, OBS_BLOCK), bf16, VMEM)],
        "gain",
        [pltpu.VMEM((rows, OBS_BLOCK), f32)],
    )(places.reshape(-1), arrived.reshape(rows, members), y, meta)

    weights = call(sweep_kernel, [VMEM] * 6, [(square, f32, VMEM)], "sweep")(
        high, low, start, w_before, start, w_after
    )
    w_before, w_after = send(weights, up), send(weights, down)
    answers = call(answer_kernel, [VMEM] * 7, [((rows, members), f32, VMEM)], "answer")(
        high, low, start, w_before, weights, w_after, gain
    )
    returned = lax.all_to_all(
        answers.reshape(devices, CAP, lines, members), AXES, 0, 0, tiled=True
    )
    return call(collect_kernel, [SMEM, VMEM, VMEM], [((tiles, lines, members), f32, VMEM)], "collect")(
        slot, prior_states, returned.reshape(slots, lines, members)
    )


def solution(mesh):
    atm, ocn = mesh.shape["atm"], mesh.shape["ocn"]
    home = homes(atm, ocn) if RELOCATE else list(range(atm * ocn))
    placed = (
        P(AXES, None, None),
        P(AXES),
        P(AXES, None),
        P(AXES, None),
        P(AXES, None),
        P(AXES),
        P(AXES),
    )
    return jax.shard_map(
        functools.partial(shards, home),
        mesh=mesh,
        in_specs=placed,
        out_specs=P(AXES, None, None),
        check_vma=False,
    )
```

```python
import functools

import jax
import jax.numpy as jnp
from jax import lax
from jax.experimental import pallas as pl
from jax.experimental.pallas import tpu as pltpu
from jax.sharding import PartitionSpec as P


OBS_BLOCK = 512
READS = 5
CAP = 2
LENGTH = 16384
LANES = 128
PARTS = OBS_BLOCK // LANES
AXES = ("atm", "ocn")
RELOCATE = True


def homes(atm, ocn):
    places = []
    for column in range(atm // 2):
        chips = range(ocn) if column % 2 == 0 else range(ocn - 1, -1, -1)
        for chip in chips:
            for core in range(2):
                places.append((2 * column + core) * ocn + chip)
    return places


def as_row(ref, start):
    return jnp.concatenate([ref[start + i : start + i + 1, :] for i in range(PARTS)], axis=1)


def as_column(ref, start, part):
    shape = (LANES, LANES)
    diagonal = lax.broadcasted_iota(jnp.int32, shape, 0) == lax.broadcasted_iota(jnp.int32, shape, 1)
    row = jnp.broadcast_to(ref[start + part : start + part + 1, :], shape)
    return jnp.sum(jnp.where(diagonal, row, 0.0), axis=1, keepdims=True)


def split(values):
    high = values.astype(jnp.bfloat16)
    return high, (values - high.astype(jnp.float32)).astype(jnp.bfloat16)


def start_kernel(inverse, y_ref, place_ref, error_ref, target_ref, weights_ref, meta_ref):
    meta_ref[:PARTS, :] = place_ref[...].astype(jnp.float32)
    meta_ref[PARTS:, :] = error_ref[...]
    for part in range(PARTS):
        rows = pl.ds(part * LANES, LANES)
        y = y_ref[rows, :].astype(jnp.float32)
        divisor = jnp.sum(y * y, axis=1, keepdims=True) * inverse + as_column(error_ref, 0, part)
        weights_ref[rows, :] = target_ref[rows, :] / divisor


def couple_kernel(
    inverse, first, last, me_ref, y_ref, before_ref, after_ref, meta_ref, meta_before_ref, meta_after_ref,
    own_high_ref, own_low_ref, near_high_ref, near_low_ref,
):
    near = ((before_ref, meta_before_ref, first), (after_ref, meta_after_ref, last))
    for part in range(PARTS):
        rows = pl.ds(part * LANES, LANES)
        y = y_ref[rows, :]
        wide = y.astype(jnp.float32)
        divisor = jnp.sum(wide * wide, axis=1, keepdims=True) * inverse + as_column(meta_ref, PARTS, part)
        place = as_column(meta_ref, 0, part)

        def coupling(other_ref, other_meta_ref):
            product = lax.dot_general(
                y, other_ref[...], (((1,), (1,)), ((), ())), preferred_element_type=jnp.float32
            )
            spread = (place - as_row(other_meta_ref, 0)) * (1.0 / LENGTH)
            return product * (-inverse / (divisor * (1.0 + spread * spread)))

        shape = (LANES, OBS_BLOCK)
        line = lax.broadcasted_iota(jnp.int32, shape, 0) + part * LANES
        own = jnp.where(line == lax.broadcasted_iota(jnp.int32, shape, 1), 0.0, coupling(y_ref, meta_ref))
        own_high_ref[rows, :], own_low_ref[rows, :] = split(own)
        for number, (other_ref, other_meta_ref, absent) in enumerate(near):
            columns = pl.ds(number * OBS_BLOCK, OBS_BLOCK)
            value = jnp.where(me_ref[0] != absent, coupling(other_ref, other_meta_ref), 0.0)
            near_high_ref[rows, columns], near_low_ref[rows, columns] = split(value)


def product(left_ref, right):
    return jnp.dot(left_ref[...], right, preferred_element_type=jnp.float32)


def own_start_kernel(high_ref, low_ref, weights_ref, part_ref):
    high, low = split(weights_ref[...])
    part_ref[...] = product(high_ref, high) + product(low_ref, high) + product(high_ref, low)


def sweep_kernel(high_ref, low_ref, before_ref, after_ref, start_ref, part_ref, weights_ref, step_ref, rest_ref):
    high, low = split(jnp.concatenate([before_ref[...], after_ref[...]], axis=0))
    change = part_ref[...] + product(high_ref, high) + product(low_ref, high) + product(high_ref, low)
    weights_ref[...] = start_ref[...] + change
    step_ref[...], rest_ref[...] = split(change)


def own_step_kernel(high_ref, low_ref, step_ref, rest_ref, weights_ref, part_ref):
    step = step_ref[...]
    part_ref[...] = (
        weights_ref[...] + product(high_ref, step) + product(low_ref, step) + product(high_ref, rest_ref[...])
    )


def answer_kernel(high_ref, low_ref, before_ref, after_ref, part_ref, gain_ref, answer_ref):
    step = jnp.concatenate([before_ref[...], after_ref[...]], axis=0)
    weights = part_ref[...] + product(high_ref, step) + product(low_ref, step)
    answer_ref[...] = product(gain_ref, weights.astype(jnp.bfloat16))


def gain_kernel(inverse, rows_ref, slabs_ref, y_ref, meta_ref, gain_ref, product_ref):
    product_ref[...] = lax.dot_general(
        rows_ref[...], y_ref[...], (((1,), (1,)), ((), ())), preferred_element_type=jnp.float32
    )
    lines = slabs_ref.shape[2]
    height = CAP * lines
    here = as_row(meta_ref, 0)

    def group(number, carry):
        places = slabs_ref[number, CAP].astype(jnp.float32)
        scales = []
        for slot in range(CAP):
            place = places[2 * slot : 2 * slot + 1, :LANES] * 256.0 + places[2 * slot + 1 : 2 * slot + 2, :LANES]
            spread = (jnp.concatenate([place] * PARTS, axis=1) - here) * (1.0 / LENGTH)
            scale = inverse / (1.0 + spread * spread)
            scales.append(jnp.broadcast_to(scale, (lines, OBS_BLOCK)))
        source = pl.ds(pl.multiple_of(number * (CAP + 1) * lines, lines), height)
        rows = pl.ds(pl.multiple_of(number * height, height), height)
        gain = product_ref[source, :] * jnp.concatenate(scales, axis=0)
        gain_ref[rows, :] = gain.astype(jnp.bfloat16)
        return carry

    lax.fori_loop(0, slabs_ref.shape[0], group, 0, unroll=4)


def request_kernel(home_ref, reads_ref, place_ref, prior_ref, send_ref, slot_ref, count_ref, at_ref):
    tiles, lines, members = prior_ref.shape
    devices = send_ref.shape[0]
    send_ref[...] = jnp.zeros_like(send_ref)

    def clear(number, carry):
        for slot in range(CAP):
            at_ref[number * CAP + slot] = 0
        count_ref[number] = 0
        return carry

    lax.fori_loop(0, devices, clear, 0)

    def tile(number, carry):
        states = prior_ref[number].astype(jnp.float32)
        mean = jnp.sum(states, axis=1, keepdims=True) * (1.0 / members)
        anomalies = (states - mean).astype(send_ref.dtype)
        for read in range(READS):
            block = home_ref[reads_ref[number, read]]
            used = jnp.minimum(count_ref[block], CAP - 1)
            count_ref[block] = used + 1
            send_ref[block, used] = anomalies
            at_ref[block * CAP + used] = place_ref[number]
            slot_ref[number * READS + read] = block * CAP + used
        return carry

    lax.fori_loop(0, tiles, tile, 0)
    line = lax.broadcasted_iota(jnp.int32, (lines, members), 0)

    def place(number, carry):
        value = jnp.zeros((lines, members), jnp.int32)
        for slot in range(CAP):
            at = at_ref[number * CAP + slot]
            value = jnp.where(line == 2 * slot, at // 256, value)
            value = jnp.where(line == 2 * slot + 1, at % 256, value)
        send_ref[number, CAP] = value.astype(jnp.float32).astype(send_ref.dtype)
        return carry

    lax.fori_loop(0, devices, place, 0)


def collect_kernel(slot_ref, prior_ref, returned_ref, out_ref):
    def tile(number, carry):
        total = returned_ref[slot_ref[number * READS]]
        for read in range(1, READS):
            total = total + returned_ref[slot_ref[number * READS + read]]
        out_ref[number] = prior_ref[number].astype(jnp.float32) + total
        return carry

    lax.fori_loop(0, prior_ref.shape[0], tile, 0)


VMEM = pl.BlockSpec(memory_space=pltpu.VMEM)
SMEM = pl.BlockSpec(memory_space=pltpu.SMEM)


def call(kernel, ins, outs, scratch=()):
    shapes = [jax.ShapeDtypeStruct(shape, dtype) for shape, dtype, _ in outs]
    specs = [space for _, _, space in outs]
    single = len(outs) == 1
    return pl.pallas_call(
        kernel,
        in_specs=list(ins),
        out_shape=shapes[0] if single else shapes,
        out_specs=specs[0] if single else specs,
        scratch_shapes=list(scratch),
    )


def shards(
    home,
    prior_states,
    patch_mesh_location,
    fetched_blocks,
    measured_deviations,
    departure_vectors,
    measurement_error_spread,
    measurement_mesh_location,
):
    f32, bf16, i32 = jnp.float32, jnp.bfloat16, jnp.int32
    tiles, lines, members = prior_states.shape
    inverse = 1.0 / (members - 1)
    devices = len(home)
    slots = devices * CAP
    rows = slots * lines
    after = home[1:] + home[:1]
    before = home[-1:] + home[:-1]
    source = list(range(devices))
    up, down = list(zip(home, after)), list(zip(home, before))

    def send(values, pairs):
        return lax.ppermute(values, AXES, pairs)

    square = (OBS_BLOCK, members)
    y = send(measured_deviations, list(zip(source, home)))
    start, meta_here = call(
        functools.partial(start_kernel, inverse), [VMEM] * 4,
        [(square, f32, VMEM), ((2 * PARTS, LANES), f32, VMEM)],
    )(
        measured_deviations,
        measurement_mesh_location.reshape(PARTS, LANES),
        measurement_error_spread.reshape(PARTS, LANES),
        departure_vectors,
    )
    start = send(start, list(zip(source, home)))
    meta = send(meta_here, list(zip(source, home)))
    meta_before = send(meta_here, list(zip(source, after)))
    meta_after = send(meta_here, list(zip(source, before)))
    slabs = (devices, CAP + 1, lines, members)
    send_rows, slot = call(
        request_kernel,
        [SMEM, SMEM, SMEM, VMEM],
        [(slabs, bf16, VMEM), ((tiles * READS,), i32, SMEM)],
        [pltpu.SMEM((devices,), i32), pltpu.SMEM((slots,), i32)],
    )(jnp.asarray(home, i32), fetched_blocks, patch_mesh_location, prior_states)
    y_before, y_after = send(y, up), send(y, down)

    me = lax.axis_index(AXES).astype(i32).reshape(1)
    own_square, near_wide = (OBS_BLOCK, OBS_BLOCK), (OBS_BLOCK, 2 * OBS_BLOCK)
    own_high, own_low, near_high, near_low = call(
        functools.partial(couple_kernel, inverse, home[0], home[-1]),
        [SMEM] + [VMEM] * 6,
        [(own_square, bf16, VMEM)] * 2 + [(near_wide, bf16, VMEM)] * 2,
    )(me, y, y_before, y_after, meta, meta_before, meta_after)
    w_before, w_after = send(start, up), send(start, down)
    part = call(own_start_kernel, [VMEM] * 3, [(square, f32, VMEM)])(own_high, own_low, start)
    arrived = lax.all_to_all(send_rows, AXES, 0, 0, tiled=True)
    weights, step, rest = call(
        sweep_kernel, [VMEM] * 6,
        [(square, f32, VMEM), (square, bf16, VMEM), (square, bf16, VMEM)],
    )(near_high, near_low, w_before, w_after, start, part)
    step_before, step_after = send(step, up), send(step, down)
    part = call(own_step_kernel, [VMEM] * 5, [(square, f32, VMEM)])(
        own_high, own_low, step, rest, weights
    )
    gain = call(
        functools.partial(gain_kernel, inverse),
        [VMEM] * 4,
        [((rows, OBS_BLOCK), bf16, VMEM)],
        [pltpu.VMEM((devices * (CAP + 1) * lines, OBS_BLOCK), f32)],
    )(arrived.reshape(-1, members), arrived, y, meta)
    answers = call(answer_kernel, [VMEM] * 6, [((rows, members), f32, VMEM)])(
        near_high, near_low, step_before, step_after, part, gain
    )
    size = jnp.sqrt(jnp.abs(answers)) * (1.0 / 16)
    coded = jnp.where(answers < 0, -size, size).astype(jnp.float16)
    returned = lax.all_to_all(
        coded.reshape(devices, CAP, lines, members), AXES, 0, 0, tiled=True
    ).astype(f32)
    returned = returned * jnp.abs(returned) * 256.0
    return call(collect_kernel, [SMEM, VMEM, VMEM], [((tiles, lines, members), f32, VMEM)])(
        slot, prior_states, returned.reshape(slots, lines, members)
    )


def solution(mesh):
    atm, ocn = mesh.shape["atm"], mesh.shape["ocn"]
    home = homes(atm, ocn) if RELOCATE else list(range(atm * ocn))
    placed = (
        P(AXES, None, None),
        P(AXES),
        P(AXES, None),
        P(AXES, None),
        P(AXES, None),
        P(AXES),
        P(AXES),
    )

    def body(*arrays):
        return shards(home, *arrays)

    return jax.shard_map(
        body,
        mesh=mesh,
        in_specs=placed,
        out_specs=P(AXES, None, None),
        check_vma=False,
    )
```

```python
import functools

import jax
import jax.numpy as jnp
from jax import lax
from jax.experimental import pallas as pl
from jax.experimental.pallas import tpu as pltpu
from jax.sharding import PartitionSpec as P


OBS_BLOCK = 512
READS = 5
CAP = 2
LENGTH = 16384
LANES = 128
PARTS = OBS_BLOCK // LANES
EXTRA = 8
AXES = ("atm", "ocn")
RELOCATE = True


def homes(atm, ocn):
    places = []
    for column in range(atm // 2):
        chips = range(ocn) if column % 2 == 0 else range(ocn - 1, -1, -1)
        for chip in chips:
            for core in range(2):
                places.append((2 * column + core) * ocn + chip)
    return places


def as_row(ref, start):
    return jnp.concatenate([ref[start + i : start + i + 1, :] for i in range(ref_rows(ref))], axis=1)


def ref_rows(ref):
    return OBS_BLOCK // ref.shape[1]


def as_column(ref, start, part):
    shape = (LANES, LANES)
    diagonal = lax.broadcasted_iota(jnp.int32, shape, 0) == lax.broadcasted_iota(jnp.int32, shape, 1)
    line, lane = divmod(part * LANES, ref.shape[1])
    row = jnp.broadcast_to(ref[start + line : start + line + 1, lane : lane + LANES], shape)
    return jnp.sum(jnp.where(diagonal, row, 0.0), axis=1, keepdims=True)


def split(values):
    high = values.astype(jnp.bfloat16)
    return high, (values - high.astype(jnp.float32)).astype(jnp.bfloat16)


def start_kernel(inverse, y_ref, place_ref, error_ref, target_ref, weights_ref):
    members = weights_ref.shape[1]
    weights_ref[OBS_BLOCK:, :] = jnp.zeros((EXTRA, members), jnp.float32)
    for part in range(PARTS):
        line, lane = divmod(part * LANES, members)
        line, lanes = OBS_BLOCK + line, pl.ds(lane, LANES)
        weights_ref[line : line + 1, lanes] = place_ref[part : part + 1, :].astype(jnp.float32)
        line = line + OBS_BLOCK // members
        weights_ref[line : line + 1, lanes] = error_ref[part : part + 1, :]
        rows = pl.ds(part * LANES, LANES)
        y = y_ref[rows, :].astype(jnp.float32)
        divisor = jnp.sum(y * y, axis=1, keepdims=True) * inverse + as_column(error_ref, 0, part)
        weights_ref[rows, :] = target_ref[rows, :] / divisor


def coupling(inverse, part, y_ref, meta_ref, other_ref, other_meta_ref):
    y = y_ref[pl.ds(part * LANES, LANES), :]
    wide = y.astype(jnp.float32)
    error = as_column(meta_ref, OBS_BLOCK + ref_rows(meta_ref), part)
    divisor = jnp.sum(wide * wide, axis=1, keepdims=True) * inverse + error
    product = lax.dot_general(
        y, other_ref[...], (((1,), (1,)), ((), ())), preferred_element_type=jnp.float32
    )
    spread = (as_column(meta_ref, OBS_BLOCK, part) - as_row(other_meta_ref, OBS_BLOCK)) * (1.0 / LENGTH)
    return product * (-inverse / (divisor * (1.0 + spread * spread)))


def product(left_ref, right):
    return jnp.dot(left_ref[...], right, preferred_element_type=jnp.float32)


def own_kernel(inverse, y_ref, start_ref, high_ref, low_ref, part_ref, meta_ref):
    for part in range(PARTS):
        shape = (LANES, OBS_BLOCK)
        line = lax.broadcasted_iota(jnp.int32, shape, 0) + part * LANES
        value = coupling(inverse, part, y_ref, start_ref, y_ref, start_ref)
        value = jnp.where(line == lax.broadcasted_iota(jnp.int32, shape, 1), 0.0, value)
        rows = pl.ds(part * LANES, LANES)
        high_ref[rows, :], low_ref[rows, :] = split(value)
    meta_ref[...] = start_ref[OBS_BLOCK:, :]
    high, low = split(start_ref[:OBS_BLOCK, :])
    part_ref[...] = product(high_ref, high) + product(low_ref, high) + product(high_ref, low)


def sweep_kernel(
    inverse, first, last, me_ref, y_ref, y_before_ref, y_after_ref, start_ref, before_ref, after_ref, part_ref,
    high_ref, low_ref, weights_ref, step_ref, rest_ref,
):
    near = ((y_before_ref, before_ref, first), (y_after_ref, after_ref, last))
    for part in range(PARTS):
        rows = pl.ds(part * LANES, LANES)
        for number, (other_ref, other_meta_ref, absent) in enumerate(near):
            columns = pl.ds(number * OBS_BLOCK, OBS_BLOCK)
            value = coupling(inverse, part, y_ref, start_ref, other_ref, other_meta_ref)
            value = jnp.where(me_ref[0] != absent, value, 0.0)
            high_ref[rows, columns], low_ref[rows, columns] = split(value)
    high, low = split(jnp.concatenate([before_ref[:OBS_BLOCK, :], after_ref[:OBS_BLOCK, :]], axis=0))
    change = part_ref[...] + product(high_ref, high) + product(low_ref, high) + product(high_ref, low)
    weights_ref[...] = start_ref[:OBS_BLOCK, :] + change
    step_ref[...], rest_ref[...] = split(change)


def own_step_kernel(high_ref, low_ref, step_ref, rest_ref, weights_ref, part_ref):
    step = step_ref[...]
    part_ref[...] = (
        weights_ref[...] + product(high_ref, step) + product(low_ref, step) + product(high_ref, rest_ref[...])
    )


def answer_kernel(high_ref, low_ref, before_ref, after_ref, part_ref, gain_ref, answer_ref):
    step = jnp.concatenate([before_ref[...], after_ref[...]], axis=0)
    weights = part_ref[...] + product(high_ref, step) + product(low_ref, step)
    answer_ref[...] = product(gain_ref, weights.astype(jnp.bfloat16))


def gain_kernel(inverse, rows_ref, slabs_ref, y_ref, meta_ref, gain_ref, product_ref):
    product_ref[...] = lax.dot_general(
        rows_ref[...], y_ref[...], (((1,), (1,)), ((), ())), preferred_element_type=jnp.float32
    )
    lines = slabs_ref.shape[2]
    height = CAP * lines
    here = as_row(meta_ref, 0)

    def group(number, carry):
        places = slabs_ref[number, CAP].astype(jnp.float32)
        scales = []
        for slot in range(CAP):
            place = places[2 * slot : 2 * slot + 1, :LANES] * 256.0 + places[2 * slot + 1 : 2 * slot + 2, :LANES]
            spread = (jnp.concatenate([place] * PARTS, axis=1) - here) * (1.0 / LENGTH)
            scale = inverse / (1.0 + spread * spread)
            scales.append(jnp.broadcast_to(scale, (lines, OBS_BLOCK)))
        source = pl.ds(pl.multiple_of(number * (CAP + 1) * lines, lines), height)
        rows = pl.ds(pl.multiple_of(number * height, height), height)
        gain = product_ref[source, :] * jnp.concatenate(scales, axis=0)
        gain_ref[rows, :] = gain.astype(jnp.bfloat16)
        return carry

    lax.fori_loop(0, slabs_ref.shape[0], group, 0, unroll=4)


def request_kernel(home_ref, reads_ref, place_ref, prior_ref, send_ref, slot_ref, count_ref, at_ref):
    tiles, lines, members = prior_ref.shape
    devices = send_ref.shape[0]
    send_ref[...] = jnp.zeros_like(send_ref)

    def clear(number, carry):
        for slot in range(CAP):
            at_ref[number * CAP + slot] = 0
        count_ref[number] = 0
        return carry

    lax.fori_loop(0, devices, clear, 0)

    def tile(number, carry):
        states = prior_ref[number].astype(jnp.float32)
        mean = jnp.sum(states, axis=1, keepdims=True) * (1.0 / members)
        anomalies = (states - mean).astype(send_ref.dtype)
        for read in range(READS):
            block = home_ref[reads_ref[number, read]]
            used = jnp.minimum(count_ref[block], CAP - 1)
            count_ref[block] = used + 1
            send_ref[block, used] = anomalies
            at_ref[block * CAP + used] = place_ref[number]
            slot_ref[number * READS + read] = block * CAP + used
        return carry

    lax.fori_loop(0, tiles, tile, 0)
    line = lax.broadcasted_iota(jnp.int32, (lines, members), 0)

    def place(number, carry):
        value = jnp.zeros((lines, members), jnp.int32)
        for slot in range(CAP):
            at = at_ref[number * CAP + slot]
            value = jnp.where(line == 2 * slot, at // 256, value)
            value = jnp.where(line == 2 * slot + 1, at % 256, value)
        send_ref[number, CAP] = value.astype(jnp.float32).astype(send_ref.dtype)
        return carry

    lax.fori_loop(0, devices, place, 0)


def collect_kernel(slot_ref, prior_ref, returned_ref, out_ref):
    def tile(number, carry):
        total = returned_ref[slot_ref[number * READS]]
        for read in range(1, READS):
            total = total + returned_ref[slot_ref[number * READS + read]]
        out_ref[number] = prior_ref[number].astype(jnp.float32) + total
        return carry

    lax.fori_loop(0, prior_ref.shape[0], tile, 0)


VMEM, SMEM, FAR, FREE = "vmem", "smem", "far", "free"
SPECS = {
    VMEM: pl.BlockSpec(memory_space=pltpu.VMEM),
    SMEM: pl.BlockSpec(memory_space=pltpu.SMEM),
    FAR: pl.BlockSpec(),
    FREE: pl.BlockSpec(),
}


def call(kernel, ins, outs, scratch=()):
    held = {VMEM: pltpu.VMEM, FAR: pltpu.HBM}
    shapes = [held.get(space, jax.ShapeDtypeStruct)(shape, dtype) for shape, dtype, space in outs]
    specs = [SPECS[space] for _, _, space in outs]
    single = len(outs) == 1
    run = pl.pallas_call(
        kernel,
        in_specs=[SPECS[space] for space in ins],
        out_shape=shapes[0] if single else shapes,
        out_specs=specs[0] if single else specs,
        scratch_shapes=list(scratch),
        compiler_params=pltpu.CompilerParams(vmem_limit_bytes=24 << 20),
    )

    def on_chip(*operands):
        return run(
            *(
                pltpu.with_memory_space_constraint(operand, held[space]) if space in held else operand
                for operand, space in zip(operands, ins)
            )
        )

    return on_chip


def shards(
    home,
    prior_states,
    patch_mesh_location,
    fetched_blocks,
    measured_deviations,
    departure_vectors,
    measurement_error_spread,
    measurement_mesh_location,
):
    f32, bf16, i32 = jnp.float32, jnp.bfloat16, jnp.int32
    tiles, lines, members = prior_states.shape
    inverse = 1.0 / (members - 1)
    devices = len(home)
    slots = devices * CAP
    rows = slots * lines
    after = home[1:] + home[:1]
    before = home[-1:] + home[:-1]
    source = list(range(devices))
    up, down = list(zip(home, after)), list(zip(home, before))

    def send(values, pairs):
        return lax.ppermute(values, AXES, pairs)

    square = (OBS_BLOCK, members)
    y = send(measured_deviations, list(zip(source, home)))
    tall = (OBS_BLOCK + EXTRA, members)
    start = call(functools.partial(start_kernel, inverse), [FAR, FREE, FREE, FAR], [(tall, f32, VMEM)])(
        measured_deviations,
        measurement_mesh_location.reshape(PARTS, LANES),
        measurement_error_spread.reshape(PARTS, LANES),
        departure_vectors,
    )
    start = send(start, list(zip(source, home)))
    slabs = (devices, CAP + 1, lines, members)
    send_rows, slot = call(
        request_kernel,
        [SMEM, SMEM, SMEM, VMEM],
        [(slabs, bf16, FAR), ((tiles * READS,), i32, SMEM)],
        [pltpu.SMEM((devices,), i32), pltpu.SMEM((slots,), i32)],
    )(jnp.asarray(home, i32), fetched_blocks, patch_mesh_location, prior_states)
    y_before, y_after = send(y, up), send(y, down)

    w_before, w_after = send(start, up), send(start, down)
    me = lax.axis_index(AXES).astype(i32).reshape(1)
    own_square, near_wide = (OBS_BLOCK, OBS_BLOCK), (OBS_BLOCK, 2 * OBS_BLOCK)
    own_high, own_low, part, meta = call(
        functools.partial(own_kernel, inverse), [VMEM] * 2,
        [(own_square, bf16, FAR)] * 2 + [(square, f32, VMEM)] + [((EXTRA, members), f32, VMEM)],
    )(y, start)
    arrived = lax.all_to_all(send_rows, AXES, 0, 0, tiled=True)
    near_high, near_low, weights, step, rest = call(
        functools.partial(sweep_kernel, inverse, home[0], home[-1]),
        [SMEM, VMEM, FAR, FAR, VMEM, FAR, FAR, VMEM],
        [(near_wide, bf16, VMEM)] * 2 + [(square, f32, VMEM)] + [(square, bf16, VMEM)] * 2,
    )(me, y, y_before, y_after, start, w_before, w_after, part)
    step_before, step_after = send(step, up), send(step, down)
    part = call(own_step_kernel, [FAR] * 2 + [VMEM] * 3, [(square, f32, VMEM)])(own_high, own_low, step, rest, weights)
    gain = call(
        functools.partial(gain_kernel, inverse),
        [FAR] * 2 + [VMEM] * 2,
        [((rows, OBS_BLOCK), bf16, VMEM)],
        [pltpu.VMEM((devices * (CAP + 1) * lines, OBS_BLOCK), f32)],
    )(arrived.reshape(-1, members), arrived, y, meta)
    answers = call(answer_kernel, [VMEM] * 6, [((rows, members), f32, VMEM)])(
        near_high, near_low, step_before, step_after, part, gain
    )
    size = jnp.sqrt(jnp.abs(answers)) * (1.0 / 16)
    coded = jnp.where(answers < 0, -size, size).astype(jnp.float16)
    returned = lax.all_to_all(
        coded.reshape(devices, CAP, lines, members), AXES, 0, 0, tiled=True
    ).astype(f32)
    returned = returned * jnp.abs(returned) * 256.0
    return call(collect_kernel, [SMEM, VMEM, VMEM], [((tiles, lines, members), f32, FREE)])(
        slot, prior_states, returned.reshape(slots, lines, members)
    )


def solution(mesh):
    atm, ocn = mesh.shape["atm"], mesh.shape["ocn"]
    home = homes(atm, ocn) if RELOCATE else list(range(atm * ocn))
    placed = (
        P(AXES, None, None),
        P(AXES),
        P(AXES, None),
        P(AXES, None),
        P(AXES, None),
        P(AXES),
        P(AXES),
    )

    def body(*arrays):
        return shards(home, *arrays)

    return jax.shard_map(
        body,
        mesh=mesh,
        in_specs=placed,
        out_specs=P(AXES, None, None),
        check_vma=False,
    )
```
